32 devices in a mesh: dp: 8 (over z, y), row: 2 (over core), col: 2 (over x).
Axes of the slice: x: 2, y: 2, z: 4, core: 2. Of those that a mesh axis runs over, the one named last changes fastest.
Arguments:
- tokens: bfloat16 [32768, 768], P(('dp', 'col'), 'row'), may hold values from -6 to 6
- w_query: float32 [768, 768], P('row', 'col'), may hold values from -0.21875 to 0.21875
- w_key: float32 [768, 768], P('row', 'col'), may hold values from -0.21875 to 0.21875
- w_value: float32 [768, 768], P('row', 'col'), may hold values from -0.21875 to 0.21875
- w_attn_out: float32 [768, 768], P('col', 'row'), may hold values from -0.875 to 0.875
- w_inter: float32 [768, 3072], P('row', 'col'), may hold values from -0.21875 to 0.21875
- w_ffout: float32 [3072, 768], P('col', 'row'), may hold values from -0.109375 to 0.109375
- b_query: float32 [768], replicated, may hold values from -3 to 3
- b_value: float32 [768], replicated, may hold values from -3 to 3
- b_attn_out: float32 [768], replicated, may hold values from -3 to 3
- b_inter: float32 [3072], replicated, may hold values from -3 to 3
- b_ffout: float32 [768], replicated, may hold values from -3 to 3
- gain_one: float32 [768], replicated, may hold values from 0.25 to 1.75
- shift_one: float32 [768], replicated, may hold values from -3 to 3
- gain_two: float32 [768], replicated, may hold values from 0.25 to 1.75
- shift_two: float32 [768], replicated, may hold values from -3 to 3
- lengths: int32 [16], replicated, may hold values from 1025 to 2048, as said below
- block_order: int32 [12, 2], replicated, may hold values from 0 to 1, each once within a row
- cotangent: bfloat16 [32768, 768], P(('dp', 'col'), 'row'), may hold values from -6 to 6
Outputs:
- layer_out: bfloat16 [32768, 768], P(('dp', 'col'), 'row')
- grad_tokens: float32 [32768, 768], P(('dp', 'col'), 'row')
- grad_w_query: float32 [768, 768], P('row', 'col')
- grad_w_key: float32 [768, 768], P('row', 'col')
- grad_w_value: float32 [768, 768], P('row', 'col')
- grad_w_attn_out: float32 [768, 768], P('col', 'row')
- grad_w_inter: float32 [768, 3072], P('row', 'col')
- grad_w_ffout: float32 [3072, 768], P('col', 'row')
- grad_b_query: float32 [768], replicated
- grad_b_value: float32 [768], replicated
- grad_b_attn_out: float32 [768], replicated
- grad_b_inter: float32 [3072], replicated
- grad_b_ffout: float32 [768], replicated
- grad_gain_one: float32 [768], replicated
- grad_shift_one: float32 [768], replicated
- grad_gain_two: float32 [768], replicated
- grad_shift_two: float32 [768], replicated
The draws below stay inside these ranges and needn't reach their ends.
Inputs may be any that keep to these rules, and one draw needn't show every extreme that they name: `lengths`: every sequence is longer than half of 2048; one sequence fills all 2048 slots. `block_order`: each row holds 0 and 1 once each.
All inputs are finite; a program needn't handle non-finite values.
Results may differ from the reference program's by a relative error of at most 0.02.
Values may be sent and summed in bfloat16 or wider, within the bound.
No kernel may reach another device: no remote copies, remote signals or barrier semaphores. Data moves between devices by JAX's collectives and lax.ppermute only.
A program may use at most 192 MiB of HBM per device.

```python
import jax
import jax.numpy as jnp
from jax import lax

D = 768
H = 12
HD = 64
FF = 3072
SEQ = 2048
SEQS = 16
TOKENS = 32768


def draw_lengths(key, part):
    values = jax.random.randint(key, (SEQS,), SEQ // 2 + 1, SEQ + 1)
    index = jnp.arange(SEQS)
    values = jnp.where(index == 0, SEQ, jnp.where(index == 1, SEQ // 2 + 1, values))
    return values.astype(jnp.int32)


def level_of(key, extent, cuts, smallest, high):
    factor_of, own = 1.0, jax.random.fold_in(key, 6)
    for axis_at, blocks in cuts:
        draws = jnp.exp(jax.random.uniform(jax.random.fold_in(own, axis_at), (blocks,), jnp.float32, smallest / len(cuts), high / len(cuts)))
        factor_of = factor_of * jnp.repeat(draws, extent[axis_at] // blocks).reshape([-1 if axis == axis_at else 1 for axis in range(len(extent))])
    return factor_of


def normal_values(rng, extent, width, reach, split=(), dtype=jnp.bfloat16):
    result = jax.random.normal(rng, extent, jnp.float32) * width
    if len(split) > 0:
        result = level_of(rng, extent, split, -0.22, 0.18) * result
    return jnp.clip(result, min=-reach, max=reach).astype(dtype)


def setup_inputs(seed: int = 0) -> dict:
    keys = jax.random.split(jax.random.key(seed), 20)
    return {
        "tokens": normal_values(keys[0], (TOKENS, D), 1.0, 6.0, ((0, 16), (1, 2))),
        "w_query": normal_values(keys[1], (D, D), D ** -0.5, 0.21875, ((0, 2), (1, 2)), jnp.float32),
        "w_key": normal_values(keys[2], (D, D), D ** -0.5, 0.21875, ((0, 2), (1, 2)), jnp.float32),
        "w_value": normal_values(keys[3], (D, D), D ** -0.5, 0.21875, ((0, 2), (1, 2)), jnp.float32),
        "w_attn_out": normal_values(keys[4], (D, D), (D // 16) ** -0.5, 0.875, ((0, 2), (1, 2)), jnp.float32),
        "w_inter": normal_values(keys[5], (D, FF), D ** -0.5, 0.21875, ((0, 2), (1, 2)), jnp.float32),
        "w_ffout": normal_values(keys[6], (FF, D), FF ** -0.5, 0.109375, ((0, 2), (1, 2)), jnp.float32),
        "b_query": normal_values(keys[7], (D,), 0.5, 3.0, (), jnp.float32),
        "b_value": normal_values(keys[8], (D,), 0.5, 3.0, (), jnp.float32),
        "b_attn_out": normal_values(keys[9], (D,), 0.5, 3.0, (), jnp.float32),
        "b_inter": normal_values(keys[10], (FF,), 0.5, 3.0, (), jnp.float32),
        "b_ffout": normal_values(keys[11], (D,), 0.5, 3.0, (), jnp.float32),
        "gain_one": jnp.clip(1.0 + 0.15 * jax.random.normal(keys[12], (D,), jnp.float32), 0.25, 1.75),
        "shift_one": normal_values(keys[13], (D,), 0.5, 3.0, (), jnp.float32),
        "gain_two": jnp.clip(1.0 + 0.15 * jax.random.normal(keys[14], (D,), jnp.float32), 0.25, 1.75),
        "shift_two": normal_values(keys[15], (D,), 0.5, 3.0, (), jnp.float32),
        "lengths": draw_lengths(jax.random.fold_in(keys[19], 71), 0),
        "block_order": jax.vmap(lambda own: jax.random.permutation(own, 2))(jax.random.split(keys[17], H)).reshape((H, 2)).astype(jnp.int32),
        "cotangent": normal_values(keys[18], (TOKENS, D), 1.0, 6.0, ((0, 16), (1, 2))),
    }


@jax.custom_vjp
def reduced_precision_input(v):
    return lax.optimization_barrier(v.astype(jnp.bfloat16)).astype(jnp.float32)

@jax.custom_vjp
def low_back(v):
    return v

def low_keep(v):
    return (reduced_precision_input(v), None)

def low_pass(kept, grad):
    return (grad,)

def back_keep(v):
    return (v, None)

def back_low(kept, grad):
    return (reduced_precision_input(grad),)
reduced_precision_input.defvjp(low_keep, low_pass)
low_back.defvjp(back_keep, back_low)
accurate_result = lax.Precision.HIGHEST
eps_norm = 1e-05
masked_score = -1e+30

def matmul(left, right):
    return jnp.dot(left, right, precision=accurate_result, preferred_element_type=jnp.float32)

def layer_norm(values, gain, shift):
    mean = lax.optimization_barrier(jnp.mean(values, axis=-1, keepdims=True))
    centered = values - mean
    variance = lax.optimization_barrier(jnp.mean(centered * centered, axis=-1, keepdims=True))
    return centered * lax.rsqrt(variance + eps_norm) * gain + shift

def attend_head(query, key, value, order, length):
    half = SEQ // 2
    blocked_query_rows = query.reshape(2, half, HD)
    blocked_key_rows = key.reshape(2, half, HD)[order]
    blocked_value_rows = value.reshape(2, half, HD)[order]
    unscaled_scores = jnp.einsum('xcr,xlr->xcl', blocked_query_rows, blocked_key_rows, precision=accurate_result)
    unscaled_scores = low_back(unscaled_scores)
    positions = order[:, None] * half + jnp.arange(half)[None, :]
    live = positions < length
    scores = jnp.where(live[:, None, :], unscaled_scores * HD ** (-0.5), masked_score)
    shifted = scores - lax.optimization_barrier(jnp.max(scores, axis=-1, keepdims=True))
    expo = jnp.exp(shifted)
    attention_probabilities = expo / lax.optimization_barrier(jnp.sum(expo, axis=-1, keepdims=True))
    blended_attention_output = jnp.einsum('lcr,lrd->lcd', reduced_precision_input(attention_probabilities), blocked_value_rows, precision=accurate_result)
    return blended_attention_output.reshape(SEQ, HD)

def attend_item(item):
    return attend_head(item[0], item[1], item[2], item[3], item[4])

def split_heads(values):
    return values.reshape(2, SEQ, H, HD).transpose(0, 2, 1, 3).reshape(2 * H, SEQ, HD)

def layer(pair_tokens, params, pair_lengths, block_order):
    w_query, w_key, w_value, w_attn_out, w_inter, w_ffout, b_query, b_value, b_attn_out, b_inter, b_ffout, gain_one, shift_one, gain_two, shift_two = params
    rows = pair_tokens.reshape(2 * SEQ, D)
    inputs = reduced_precision_input(rows)
    query = reduced_precision_input(low_back(matmul(inputs, reduced_precision_input(w_query)) + b_query))
    key = reduced_precision_input(low_back(matmul(inputs, reduced_precision_input(w_key))))
    value = reduced_precision_input(low_back(matmul(inputs, reduced_precision_input(w_value)) + b_value))
    orders_all = jnp.tile(block_order, (2, 1))
    lengths_all = jnp.repeat(pair_lengths, H)
    blended_attention_output = lax.map(jax.checkpoint(attend_item), (split_heads(query), split_heads(key), split_heads(value), orders_all, lengths_all))
    merged = blended_attention_output.reshape(2, H, SEQ, HD).transpose(0, 2, 1, 3).reshape(2 * SEQ, D)
    attended = reduced_precision_input(low_back(merged))
    residual_one = rows + low_back(matmul(attended, reduced_precision_input(w_attn_out))) + b_attn_out
    normed_one = layer_norm(residual_one, gain_one, shift_one)
    hidden_pre = low_back(matmul(reduced_precision_input(normed_one), reduced_precision_input(w_inter)) + b_inter)
    hidden = reduced_precision_input(jax.nn.gelu(hidden_pre, approximate=False))
    residual_two = normed_one + low_back(matmul(hidden, reduced_precision_input(w_ffout))) + b_ffout
    return layer_norm(residual_two, gain_two, shift_two)

def reference(tokens, w_query, w_key, w_value, w_attn_out, w_inter, w_ffout, b_query, b_value, b_attn_out, b_inter, b_ffout, gain_one, shift_one, gain_two, shift_two, lengths, block_order, cotangent):
    params = (w_query, w_key, w_value, w_attn_out, w_inter, w_ffout, b_query, b_value, b_attn_out, b_inter, b_ffout, gain_one, shift_one, gain_two, shift_two)
    params = tuple((p.astype(jnp.float32) for p in params))
    pairs = tokens.astype(jnp.float32).reshape(SEQS // 2, 2, SEQ, D)
    grads_out = cotangent.astype(jnp.float32).reshape(SEQS // 2, 2, SEQ, D)
    pair_lens = lengths.reshape(SEQS // 2, 2)

    def step(total, item):
        pair_tokens, grad_pair, length_pair = item
        live = (jnp.arange(SEQ)[None, :] < length_pair[:, None]).astype(jnp.float32)
        output, pullback = jax.vjp(lambda t, p: layer(t, p, length_pair, block_order), pair_tokens, params)
        grad_in, grad_params = pullback((grad_pair * live[:, :, None]).reshape(2 * SEQ, D))
        total = jax.tree.map(jnp.add, total, grad_params)
        return (total, (output, grad_in))
    start = tuple((jnp.zeros(p.shape, jnp.float32) for p in params))
    totals, (outputs, grad_ins) = lax.scan(step, start, (pairs, grads_out, pair_lens))
    layer_out = outputs.reshape(TOKENS, D).astype(jnp.bfloat16)
    grad_tokens = grad_ins.reshape(TOKENS, D)
    return (layer_out, grad_tokens, totals[0], totals[1], totals[2], totals[3], totals[4], totals[5], totals[6], totals[7], totals[8], totals[9], totals[10], totals[11], totals[12], totals[13], totals[14])
```

```python
import functools

import jax
import jax.numpy as jnp
from jax import lax
from jax.experimental import pallas as pl
from jax.experimental.pallas import tpu as pltpu
from jax.sharding import PartitionSpec as P

BF = jnp.bfloat16
F32 = jnp.float32
D = 768
WIDE = 384
HD = 64
FF = 3072
FH = 1536
SEQ = 2048
HALF = 1024
TILE = 256
QKV = 3 * WIDE

eps_norm = 1e-05
masked_score = -1e30
LOG2E = 1.4426950408889634


def dot_nn(left, right):
    return lax.dot_general(left, right, (((1,), (0,)), ((), ())), preferred_element_type=F32)


def dot_nt(left, right):
    return lax.dot_general(left, right, (((1,), (1,)), ((), ())), preferred_element_type=F32)


def side_by_side(left, right):
    return jnp.concatenate([left[...], right[...]], 1)


def flip(values, axis, bit=1):
    size = lax.axis_size(axis)
    return lax.ppermute(values, axis, [(i, i ^ bit) for i in range(size)])


def copies(pieces, whole, axis_sizes, sems):
    made = []
    for index, (piece, (row, col)) in enumerate(pieces):
        rows, cols = piece.shape
        target = whole.at[pl.ds(row, rows), pl.ds(col, cols)]
        made.append(pltpu.make_async_copy(piece, target, sems.at[index]))
    return made


def any_spec():
    return pl.BlockSpec(memory_space=pl.ANY)


def project_kernel(spot, own, oth, w_own, w_oth, bias, query, key, value, weight, sems):
    step = pl.program_id(0)

    @pl.when(step == 0)
    def _():
        made = copies([(w_own, (0, 0)), (w_oth, (WIDE, 0))], weight, None, sems)
        for item in made:
            item.start()
        for item in made:
            item.wait()

    rows = side_by_side(own, oth)
    both = dot_nn(rows, weight[:, WIDE:])
    key[...] = both[:, :WIDE].astype(BF)
    value[...] = (both[:, WIDE:] + bias[1:2, :]).astype(BF)

    @pl.when(step // (HALF // TILE) == spot[0])
    def _():
        found = dot_nn(rows, weight[:, :WIDE]) + bias[0:1, :]
        query[...] = (found * (LOG2E * HD ** (-0.5))).astype(BF)


def project(spot, own, oth, w_own, w_oth, bias):
    per = HALF // TILE
    tile = pl.BlockSpec((TILE, WIDE), lambda i, s: (i, 0))
    return pl.pallas_call(
        project_kernel,
        out_shape=(
            jax.ShapeDtypeStruct((HALF, WIDE), BF),
            jax.ShapeDtypeStruct((SEQ, WIDE), BF),
            jax.ShapeDtypeStruct((SEQ, WIDE), BF),
        ),
        grid_spec=pltpu.PrefetchScalarGridSpec(
            num_scalar_prefetch=1,
            grid=(SEQ // TILE,),
            in_specs=[
                tile,
                tile,
                any_spec(),
                any_spec(),
                pl.BlockSpec((8, WIDE), lambda i, s: (0, 0)),
            ],
            out_specs=(
                pl.BlockSpec((TILE, WIDE), lambda i, s: (jnp.clip(i - s[0] * per, 0, per - 1), 0)),
                tile,
                tile,
            ),
            scratch_shapes=[pltpu.VMEM((D, QKV), BF), pltpu.SemaphoreType.DMA((2,))],
        ),
        name="project",
    )(spot, own, oth, w_own, w_oth, bias)


def attend_forward_kernel(pick, live, query, key, value, mixed, logsum, key_s, turned_s):
    pair = pl.program_id(0)
    rows, lanes = query.shape
    lane = lax.broadcasted_iota(jnp.int32, (1, lanes), 1)
    position = lax.broadcasted_iota(jnp.int32, (HALF, 1), 0)
    for head in range(2):
        start = pl.multiple_of(pick[2 * pair + head] * HALF, HALF)
        mine = (lane >= head * HD) & (lane < (head + 1) * HD)
        part = value[pl.ds(start, HALF), :]
        turned_s[head] = jnp.where(mine, part, jnp.ones_like(part)).T
        bias = jnp.where(position + start < live[0], 0.0, masked_score).astype(BF)
        part = key[pl.ds(start, HALF), :]
        other = lane == (1 - head) * HD
        key_s[head] = jnp.where(mine, part, jnp.where(other, bias, jnp.zeros_like(part)))
    query_all = query[...]
    outs = []
    for head in range(2):
        mine = (lane >= head * HD) & (lane < (head + 1) * HD)
        query_head = jnp.where(mine, query_all, jnp.ones_like(query_all))
        scores = dot_nt(key_s[head], query_head)
        top = jnp.max(scores, 0, keepdims=True)
        expo = jnp.exp2(scores - top).astype(BF)
        blend = dot_nn(turned_s[head], expo)
        total = blend[(1 - head) * HD : (1 - head) * HD + 1, :]
        outs.append(blend[head * HD : (head + 1) * HD, :] / total)
        logsum[0, head : head + 1, :] = top + jnp.log2(total)
    mixed[...] = jnp.concatenate(outs, 0).T.astype(BF)


def attend_forward(pick, live, query, key, value):
    rows, width = query.shape
    pairs = width // 128
    return pl.pallas_call(
        attend_forward_kernel,
        out_shape=(
            jax.ShapeDtypeStruct((rows, width), BF),
            jax.ShapeDtypeStruct((pairs, 8, rows), F32),
        ),
        grid_spec=pltpu.PrefetchScalarGridSpec(
            num_scalar_prefetch=2,
            grid=(pairs,),
            in_specs=[
                pl.BlockSpec((rows, 128), lambda p, *_: (0, p)),
                pl.BlockSpec((2 * HALF, 128), lambda p, *_: (0, p)),
                pl.BlockSpec((2 * HALF, 128), lambda p, *_: (0, p)),
            ],
            out_specs=(
                pl.BlockSpec((rows, 128), lambda p, *_: (0, p)),
                pl.BlockSpec((1, 8, rows), lambda p, *_: (p, 0, 0)),
            ),
            scratch_shapes=[pltpu.VMEM((2, HALF, 128), BF), pltpu.VMEM((2, 128, HALF), BF)],
        ),
        name="attend_forward",
    )(pick, live, query, key, value)


def split_three(values):
    high = values.astype(BF)
    rest = values - high.astype(F32)
    middle = rest.astype(BF)
    return high, middle, (rest - middle.astype(F32)).astype(BF)


def attend_backward_kernel(
    pick,
    live,
    query,
    key,
    value,
    mixed,
    grad_mixed,
    logsum,
    grad_query,
    grad_key,
    grad_value,
    query_s,
    grad_s,
):
    pair = pl.program_id(0)
    rows, lanes = query.shape
    lane = lax.broadcasted_iota(jnp.int32, (1, lanes), 1)
    position = lax.broadcasted_iota(jnp.int32, (HALF, 1), 0)
    weighted = mixed[...].astype(F32) * grad_mixed[...].astype(F32)
    sums = logsum[0].T
    grad_key[...] = jnp.zeros_like(grad_key)
    grad_value[...] = jnp.zeros_like(grad_value)
    for head in range(2):
        mine = (lane >= head * HD) & (lane < (head + 1) * HD)
        base = (1 - head) * HD
        delta = jnp.sum(jnp.where(mine, weighted, 0.0), 1, keepdims=True)
        low = jnp.where(mine, grad_mixed[...], jnp.zeros_like(grad_mixed))
        for at, piece in enumerate(split_three(-delta)):
            low = jnp.where(lane == base + at, piece, low)
        grad_s[head] = low
        low = jnp.where(mine, query[...], jnp.zeros_like(query))
        for at, piece in enumerate(split_three(-sums[:, head : head + 1])):
            low = jnp.where(lane == base + at, piece, low)
        query_s[head] = jnp.where(lane == base + 3, jnp.ones_like(low), low)
    turned = jnp.zeros((lanes, rows), F32)
    for head in range(2):
        start = pl.multiple_of(pick[2 * pair + head] * HALF, HALF)
        mine = (lane >= head * HD) & (lane < (head + 1) * HD)
        base = (1 - head) * HD
        extra = (lane >= base) & (lane < base + 3)
        bias = jnp.where(position + start < live[0], 0.0, masked_score).astype(BF)
        key_tile = key[pl.ds(start, HALF), :]
        ones = jnp.ones_like(key_tile)
        zeros = jnp.zeros_like(key_tile)
        fill = jnp.where(extra, ones, jnp.where(lane == base + 3, bias, zeros))
        scores = dot_nt(jnp.where(mine, key_tile, fill), query_s[head])
        value_tile = value[pl.ds(start, HALF), :]
        grad_probs = dot_nt(
            jnp.where(mine, value_tile, jnp.where(extra, ones, zeros)), grad_s[head]
        )
        expo = jnp.exp2(scores)
        grad_scores = (expo * grad_probs).astype(BF)
        found = dot_nn(expo.astype(BF), grad_s[head]).astype(BF)
        grad_value[pl.ds(start, HALF), :] = jnp.where(
            mine, found, grad_value[pl.ds(start, HALF), :]
        )
        found = (dot_nn(grad_scores, query_s[head]) * (1.0 / LOG2E)).astype(BF)
        grad_key[pl.ds(start, HALF), :] = jnp.where(mine, found, grad_key[pl.ds(start, HALF), :])
        turned = turned + dot_nn(jnp.where(mine, key_tile, zeros).T, grad_scores)
    grad_query[...] = (turned * HD ** (-0.5)).T.astype(BF)


def attend_backward(pick, live, query, key, value, mixed, grad_mixed, logsum):
    rows, width = query.shape
    pairs = width // 128
    full = pl.BlockSpec((rows, 128), lambda p, *_: (0, p))
    both = pl.BlockSpec((2 * HALF, 128), lambda p, *_: (0, p))
    return pl.pallas_call(
        attend_backward_kernel,
        out_shape=(
            jax.ShapeDtypeStruct((rows, width), BF),
            jax.ShapeDtypeStruct((2 * HALF, width), BF),
            jax.ShapeDtypeStruct((2 * HALF, width), BF),
        ),
        grid_spec=pltpu.PrefetchScalarGridSpec(
            num_scalar_prefetch=2,
            grid=(pairs,),
            in_specs=[
                full,
                both,
                both,
                full,
                full,
                pl.BlockSpec((1, 8, rows), lambda p, *_: (p, 0, 0)),
            ],
            out_specs=(full, both, both),
            scratch_shapes=[pltpu.VMEM((2, rows, 128), BF), pltpu.VMEM((2, rows, 128), BF)],
        ),
        name="attend_backward",
    )(pick, live, query, key, value, mixed, grad_mixed, logsum)


def gelu_parts(pre):
    bell = jnp.exp2(pre * pre * (-0.5 * LOG2E))
    ratio = 1.0 / (1.0 + jnp.abs(pre) * (0.3275911 * 0.5**0.5))
    tail = 0.5 * 1.061405429 * ratio + 0.5 * -1.453152027
    tail = tail * ratio + 0.5 * 1.421413741
    tail = tail * ratio + 0.5 * -0.284496736
    tail = tail * ratio + 0.5 * 0.254829592
    tail = tail * ratio * bell
    below = jnp.where(pre > 0.0, 1.0 - tail, tail)
    return pre * below, below + pre * bell * 0.3989422804014327


def norm_rows(values):
    centred = values - jnp.mean(values, 1, keepdims=True)
    scale = lax.rsqrt(jnp.mean(centred * centred, 1, keepdims=True) + eps_norm)
    return centred * scale, scale


def norm_back(inner, normal, scale):
    plain = jnp.mean(inner, 1, keepdims=True)
    along = jnp.mean(inner * normal, 1, keepdims=True)
    return scale * (inner - plain - normal * along)


def row_sums(values):
    return jnp.sum(values, 0, keepdims=True)


def chain_forward_kernel(
    spot,
    live,
    mixed_own,
    mixed_oth,
    tok_own,
    tok_oth,
    cot_own,
    cot_oth,
    vectors,
    bias_inter,
    *rest,
):
    pieces = rest[:12]
    (
        out_own,
        out_oth,
        normed_low,
        normal_one,
        scale_one,
        hidden,
        slope,
        grad_two,
        low_own,
        low_oth,
        sums,
    ) = rest[12:23]
    w_attn, w_inter, w_ffout, sems = rest[23:]
    step = pl.program_id(0)
    spots_attn = [(0, 0), (0, WIDE), (WIDE, 0), (WIDE, WIDE)]
    spots_inter = [(0, 0), (WIDE, 0), (0, FH), (WIDE, FH)]
    spots_ffout = [(0, 0), (0, WIDE), (FH, 0), (FH, WIDE)]
    attn_copies = copies(list(zip(pieces[0:4], spots_attn)), w_attn, None, sems.at[0])
    inter_copies = copies(list(zip(pieces[4:8], spots_inter)), w_inter, None, sems.at[1])
    ffout_copies = copies(list(zip(pieces[8:12], spots_ffout)), w_ffout, None, sems.at[2])

    @pl.when(step == 0)
    def _():
        for item in attn_copies + inter_copies + ffout_copies:
            item.start()
        for item in attn_copies:
            item.wait()

    residual = (
        side_by_side(tok_own, tok_oth).astype(F32)
        + dot_nn(side_by_side(mixed_own, mixed_oth), w_attn[...])
        + vectors[0:1, :]
    )
    normal, scale = norm_rows(residual)
    normed = normal * vectors[1:2, :] + vectors[2:3, :]
    low = normed.astype(BF)
    normal_one[...] = normal
    scale_one[...] = jnp.broadcast_to(scale, scale_one.shape)
    normed_low[...] = low

    @pl.when(step == 0)
    def _():
        for item in inter_copies:
            item.wait()

    width = FH // 2
    for part in range(FF // width):
        at = slice(part * width, (part + 1) * width)
        pre = dot_nn(low, w_inter[:, at]) + bias_inter[0:1, at]
        value, factor = gelu_parts(pre)
        hidden[:, at] = value.astype(BF)
        slope[:, at] = factor.astype(BF)

    @pl.when(step == 0)
    def _():
        for item in ffout_copies:
            item.wait()

    residual = normed + dot_nn(hidden[...], w_ffout[...]) + vectors[3:4, :]
    normal, scale = norm_rows(residual)
    layer = (normal * vectors[4:5, :] + vectors[5:6, :]).astype(BF)
    out_own[...] = layer[:, :WIDE]
    out_oth[...] = layer[:, WIDE:]
    rows = lax.broadcasted_iota(jnp.int32, (TILE, 1), 0) + (spot[0] * HALF + step * TILE)
    cot = side_by_side(cot_own, cot_oth).astype(F32)
    cot = jnp.where(rows < live[0], cot, 0.0)
    grad = norm_back(cot * vectors[4:5, :], normal, scale)
    grad_two[...] = grad
    low = grad.astype(BF)
    low_own[...] = low[:, :WIDE]
    low_oth[...] = low[:, WIDE:]

    @pl.when(step == 0)
    def _():
        sums[...] = jnp.zeros_like(sums)

    sums[0:1, :] += row_sums(cot * normal)
    sums[1:2, :] += row_sums(cot)
    sums[2:3, :] += row_sums(grad)


def weight_pieces(weights):
    return [piece for weight in weights for piece in weight]


def chain_forward(spot, live, mixed, tokens, cot, vectors, bias_inter, weights):
    per = HALF // TILE
    row = lambda width: pl.BlockSpec((TILE, width), lambda i, *_: (i, 0))
    mine = pl.BlockSpec((TILE, WIDE), lambda i, s, n: (s[0] * per + i, 0))
    still = lambda rows, width: pl.BlockSpec((rows, width), lambda i, *_: (0, 0))
    shape = lambda width, kind: jax.ShapeDtypeStruct((HALF, width), kind)
    return pl.pallas_call(
        chain_forward_kernel,
        out_shape=(
            shape(WIDE, BF),
            shape(WIDE, BF),
            shape(D, BF),
            shape(D, F32),
            shape(128, F32),
            shape(FF, BF),
            shape(FF, BF),
            shape(D, F32),
            shape(WIDE, BF),
            shape(WIDE, BF),
            jax.ShapeDtypeStruct((8, D), F32),
        ),
        grid_spec=pltpu.PrefetchScalarGridSpec(
            num_scalar_prefetch=2,
            grid=(per,),
            in_specs=[
                row(WIDE),
                row(WIDE),
                mine,
                mine,
                mine,
                row(WIDE),
                still(8, D),
                still(8, FF),
            ]
            + [any_spec()] * 12,
            out_specs=(
                row(WIDE),
                row(WIDE),
                row(D),
                row(D),
                row(128),
                row(FF),
                row(FF),
                row(D),
                row(WIDE),
                row(WIDE),
                still(8, D),
            ),
            scratch_shapes=[
                pltpu.VMEM((D, D), BF),
                pltpu.VMEM((D, FF), BF),
                pltpu.VMEM((FF, D), BF),
                pltpu.SemaphoreType.DMA((3, 4)),
            ],
        ),
        name="chain_forward",
    )(spot, live, *mixed, *tokens, *cot, vectors, bias_inter, *weight_pieces(weights))


def chain_backward_kernel(vectors, grad_two, slope, normal_one, scale_one, *rest):
    pieces = rest[:12]
    (grad_pre, grad_one, low_own, low_oth, mixed_own, mixed_oth, sums, sums_inter) = rest[12:20]
    w_attn, w_inter, w_ffout, sems = rest[20:]
    step = pl.program_id(0)
    spots_attn = [(0, 0), (0, WIDE), (WIDE, 0), (WIDE, WIDE)]
    spots_inter = [(0, 0), (WIDE, 0), (0, FH), (WIDE, FH)]
    spots_ffout = [(0, 0), (0, WIDE), (FH, 0), (FH, WIDE)]
    attn_copies = copies(list(zip(pieces[0:4], spots_attn)), w_attn, None, sems.at[0])
    inter_copies = copies(list(zip(pieces[4:8], spots_inter)), w_inter, None, sems.at[1])
    ffout_copies = copies(list(zip(pieces[8:12], spots_ffout)), w_ffout, None, sems.at[2])

    @pl.when(step == 0)
    def _():
        for item in ffout_copies + inter_copies + attn_copies:
            item.start()
        sums[...] = jnp.zeros_like(sums)
        sums_inter[...] = jnp.zeros_like(sums_inter)
        for item in ffout_copies:
            item.wait()

    low = grad_two[...].astype(BF)
    width = FH // 2
    for part in range(FF // width):
        at = slice(part * width, (part + 1) * width)
        pre = (dot_nt(low, w_ffout[at, :]) * slope[:, at].astype(F32)).astype(BF)
        grad_pre[:, at] = pre
        sums_inter[0:1, at] += row_sums(pre.astype(F32))

    @pl.when(step == 0)
    def _():
        for item in inter_copies:
            item.wait()
        for item in attn_copies:
            item.wait()

    grad = grad_two[...] + dot_nt(grad_pre[...], w_inter[...])
    normal = normal_one[...]
    sums[0:1, :] += row_sums(grad * normal)
    sums[1:2, :] += row_sums(grad)
    grad = norm_back(grad * vectors[1:2, :], normal, scale_one[:, 0:1])
    sums[2:3, :] += row_sums(grad)
    grad_one[...] = grad
    low = grad.astype(BF)
    low_own[...] = low[:, :WIDE]
    low_oth[...] = low[:, WIDE:]
    back = dot_nt(low, w_attn[...]).astype(BF)
    mixed_own[...] = back[:, :WIDE]
    mixed_oth[...] = back[:, WIDE:]


def chain_backward(vectors, grad_two, slope, normal_one, scale_one, weights):
    per = HALF // TILE
    row = lambda width: pl.BlockSpec((TILE, width), lambda i: (i, 0))
    still = lambda rows, width: pl.BlockSpec((rows, width), lambda i: (0, 0))
    shape = lambda width, kind: jax.ShapeDtypeStruct((HALF, width), kind)
    return pl.pallas_call(
        chain_backward_kernel,
        out_shape=(
            shape(FF, BF),
            shape(D, F32),
            shape(WIDE, BF),
            shape(WIDE, BF),
            shape(WIDE, BF),
            shape(WIDE, BF),
            jax.ShapeDtypeStruct((8, D), F32),
            jax.ShapeDtypeStruct((8, FF), F32),
        ),
        grid_spec=pltpu.PrefetchScalarGridSpec(
            num_scalar_prefetch=0,
            grid=(per,),
            in_specs=[still(8, D), row(D), row(FF), row(D), row(128)] + [any_spec()] * 12,
            out_specs=(
                row(FF),
                row(D),
                row(WIDE),
                row(WIDE),
                row(WIDE),
                row(WIDE),
                still(8, D),
                still(8, FF),
            ),
            scratch_shapes=[
                pltpu.VMEM((D, D), BF),
                pltpu.VMEM((D, FF), BF),
                pltpu.VMEM((FF, D), BF),
                pltpu.SemaphoreType.DMA((3, 4)),
            ],
        ),
        name="chain_backward",
    )(vectors, grad_two, slope, normal_one, scale_one, *weight_pieces(weights))


def outer_tall_kernel(left, own, oth, out_own, out_oth):
    found = dot_nn(left[...].T, side_by_side(own, oth))
    out_own[...] = found[:, :WIDE].astype(BF)
    out_oth[...] = found[:, WIDE:].astype(BF)


def outer_tall(left, offset, count, tile, own, oth):
    still = pl.BlockSpec((HALF, WIDE), lambda i: (0, 0))
    made = pl.BlockSpec((tile, WIDE), lambda i: (i, 0))
    shape = jax.ShapeDtypeStruct((count * tile, WIDE), BF)
    return pl.pallas_call(
        outer_tall_kernel,
        out_shape=(shape, shape),
        grid=(count,),
        in_specs=[pl.BlockSpec((HALF, tile), lambda i: (0, offset + i)), still, still],
        out_specs=(made, made),
        name="outer_tall",
    )(left, own, oth)


def outer_wide_kernel(left, right, out_own, out_oth, turned):
    @pl.when(pl.program_id(0) == 0)
    def _():
        turned[...] = left[...].T

    found = dot_nn(turned[...], right[...])
    out_own[...] = found[:WIDE].astype(BF)
    out_oth[...] = found[WIDE:].astype(BF)


def outer_wide(left, right, offset, count, tile):
    made = pl.BlockSpec((WIDE, tile), lambda i: (0, i))
    shape = jax.ShapeDtypeStruct((WIDE, count * tile), BF)
    return pl.pallas_call(
        outer_wide_kernel,
        out_shape=(shape, shape),
        grid=(count,),
        in_specs=[
            pl.BlockSpec((HALF, D), lambda i: (0, 0)),
            pl.BlockSpec((HALF, tile), lambda i: (0, offset + i)),
        ],
        out_specs=(made, made),
        scratch_shapes=[pltpu.VMEM((D, HALF), BF)],
        name="outer_wide",
    )(left, right)


def outer_qkv_kernel(
    spot, tok_own, tok_oth, query, key, value, out_own, out_oth, sums, total
):
    step = pl.program_id(0)
    per = HALF // (2 * TILE)

    @pl.when(step == 0)
    def _():
        total[...] = jnp.zeros_like(total)
        sums[...] = jnp.zeros_like(sums)

    turned = side_by_side(tok_own, tok_oth).T
    total[:, WIDE:] += dot_nn(turned, side_by_side(key, value))
    sums[1:2, :] += row_sums(value[...].astype(F32))

    @pl.when(step // per == spot[0])
    def _():
        total[:, :WIDE] += dot_nn(turned, query[...])
        sums[0:1, :] += row_sums(query[...].astype(F32))

    @pl.when(step == pl.num_programs(0) - 1)
    def _():
        out_own[...] = total[:WIDE].astype(BF)
        out_oth[...] = total[WIDE:].astype(BF)


def outer_qkv(spot, tokens, query, key, value):
    tile = 2 * TILE
    per = HALF // tile
    row = pl.BlockSpec((tile, WIDE), lambda i, s: (i, 0))
    still = pl.BlockSpec((WIDE, QKV), lambda i, s: (0, 0))
    shape = jax.ShapeDtypeStruct((WIDE, QKV), BF)
    return pl.pallas_call(
        outer_qkv_kernel,
        out_shape=(shape, shape, jax.ShapeDtypeStruct((8, WIDE), F32)),
        grid_spec=pltpu.PrefetchScalarGridSpec(
            num_scalar_prefetch=1,
            grid=(SEQ // tile,),
            in_specs=[
                row,
                row,
                pl.BlockSpec((tile, WIDE), lambda i, s: (jnp.clip(i - s[0] * per, 0, per - 1), 0)),
                row,
                row,
            ],
            out_specs=(still, still, pl.BlockSpec((8, WIDE), lambda i, s: (0, 0))),
            scratch_shapes=[pltpu.VMEM((D, QKV), F32)],
        ),
        name="outer_qkv",
    )(spot, *tokens, query, key, value)


def unproject_kernel(
    spot,
    query_own,
    query_oth,
    key_own,
    key_oth,
    value_own,
    value_oth,
    grad_one,
    *rest,
):
    pieces = rest[:4]
    out_own, out_oth, weight, sems = rest[4:]
    step = pl.program_id(0)

    @pl.when(step == 0)
    def _():
        places = [(0, 0), (WIDE, 0), (0, QKV), (WIDE, QKV)]
        made = copies(list(zip(pieces, places)), weight, None, sems)
        for item in made:
            item.start()
        for item in made:
            item.wait()

    own = dot_nt(side_by_side(key_own, value_own), weight[:, WIDE:QKV])
    own = own + dot_nt(side_by_side(key_oth, value_oth), weight[:, QKV + WIDE :])
    here = step // (HALF // TILE) == spot[0]

    @pl.when(here)
    def _():
        found = own + grad_one[...]
        found = found + dot_nt(query_own[...], weight[:, :WIDE])
        found = found + dot_nt(query_oth[...], weight[:, QKV : QKV + WIDE])
        out_own[...] = found[:, :WIDE]
        out_oth[...] = found[:, WIDE:].astype(BF)

    @pl.when(jnp.logical_not(here))
    def _():
        out_own[...] = own[:, :WIDE]
        out_oth[...] = own[:, WIDE:].astype(BF)


def unproject(spot, query, key, value, grad_one, pieces):
    per = HALF // TILE
    row = pl.BlockSpec((TILE, WIDE), lambda i, s: (i, 0))
    clip = lambda i, s: (jnp.clip(i - s[0] * per, 0, per - 1), 0)
    mine = pl.BlockSpec((TILE, WIDE), clip)
    return pl.pallas_call(
        unproject_kernel,
        out_shape=(
            jax.ShapeDtypeStruct((SEQ, WIDE), F32),
            jax.ShapeDtypeStruct((SEQ, WIDE), BF),
        ),
        grid_spec=pltpu.PrefetchScalarGridSpec(
            num_scalar_prefetch=1,
            grid=(SEQ // TILE,),
            in_specs=[mine, mine, row, row, row, row, pl.BlockSpec((TILE, D), clip)]
            + [any_spec()] * 4,
            out_specs=(row, row),
            scratch_shapes=[pltpu.VMEM((D, 2 * QKV), BF), pltpu.SemaphoreType.DMA((4,))],
        ),
        name="unproject",
    )(spot, *query, *key, *value, grad_one, *pieces)


def added(left, right):
    return (left.astype(F32) + right.astype(F32)).astype(BF)


def sum_over_dp(values):
    size = lax.axis_size("dp")
    index = lax.axis_index("dp")
    bits = [1 << k for k in range(size.bit_length() - 1)]
    for bit in bits:
        half = values.shape[0] // 2
        upper = (index & bit) // bit
        send = lax.dynamic_slice_in_dim(values, (1 - upper) * half, half)
        keep = lax.dynamic_slice_in_dim(values, upper * half, half)
        values = added(keep, flip(send, "dp", bit))
    for bit in reversed(bits):
        other = flip(values, "dp", bit)
        upper = (index & bit) != 0
        first = jnp.where(upper, other, values)
        second = jnp.where(upper, values, other)
        values = jnp.concatenate([first, second], 0)
    return values


def sum_everywhere(values):
    for axis in ("row", "col", "dp"):
        for k in range(lax.axis_size(axis).bit_length() - 1):
            values = values + flip(values, axis, 1 << k)
    return values


def in_order(values, index, axis=-1):
    half = values.shape[axis] // 2
    first = lax.slice_in_dim(values, 0, half, axis=axis)
    second = lax.slice_in_dim(values, half, 2 * half, axis=axis)
    swapped = jnp.concatenate([second, first], axis)
    return jnp.where(index == 0, values, swapped)


def padded(rows, width):
    return jnp.concatenate([rows, jnp.zeros((8 - rows.shape[0], width), F32)], 0)


def per_device(
    tokens,
    w_query,
    w_key,
    w_value,
    w_attn_out,
    w_inter,
    w_ffout,
    b_query,
    b_value,
    b_attn_out,
    b_inter,
    b_ffout,
    gain_one,
    shift_one,
    gain_two,
    shift_two,
    lengths,
    block_order,
    cotangent,
):
    row = lax.axis_index("row")
    col = lax.axis_index("col")
    sequence = lax.axis_index("dp") * lax.axis_size("col") + col
    spot = row.reshape(1).astype(jnp.int32)
    live = lax.dynamic_slice(lengths, (sequence,), (1,)).astype(jnp.int32)
    heads = block_order.shape[0] // 2
    picks = lax.dynamic_slice(block_order, (0, row), (2 * heads, 1))[:, 0].astype(jnp.int32)
    picks = in_order(picks, col)

    qkv_0 = jnp.concatenate([w_query.astype(BF), w_key.astype(BF), w_value.astype(BF)], 1)
    qkv_1 = flip(qkv_0, "row")
    tokens_oth = flip(tokens, "row")
    qkv_2 = flip(qkv_0, "col")
    qkv_3 = flip(qkv_2, "row")
    weights = []
    for weight in (w_attn_out, w_inter, w_ffout):
        own = weight.astype(BF)
        over = flip(own, "col")
        weights.append((own, flip(own, "row"), over, flip(over, "row")))
    cot_send = lax.dynamic_slice_in_dim(cotangent, (1 - row) * HALF, HALF)
    cot_oth = flip(cot_send, "row")

    b_query = in_order(b_query, col)
    b_value = in_order(b_value, col)
    qv_bias = [
        padded(jnp.stack([b_query[:WIDE], b_value[:WIDE]]), WIDE),
        padded(jnp.stack([b_query[WIDE:], b_value[WIDE:]]), WIDE),
    ]
    vectors = jnp.stack([b_attn_out, gain_one, shift_one, b_ffout, gain_two, shift_two])
    vectors = padded(in_order(vectors, row), D)
    bias_inter = padded(in_order(b_inter, col)[None], FF)

    both = (tokens, tokens_oth)
    parts = []
    for side, (low, high) in enumerate(((qkv_0, qkv_1), (qkv_2, qkv_3))):
        pick = picks[side * heads : (side + 1) * heads]
        query, key, value = project(spot, *both, low, high, qv_bias[side])
        mixed, logsum = attend_forward(pick, live, query, key, value)
        parts.append((pick, query, key, value, mixed, logsum))

    (
        out_own,
        out_oth,
        normed,
        normal_one,
        scale_one,
        hidden,
        slope,
        grad_two,
        two_own,
        two_oth,
        sums_two,
    ) = chain_forward(
        spot,
        live,
        (parts[0][4], parts[1][4]),
        both,
        (cotangent, cot_oth),
        vectors,
        bias_inter,
        weights,
    )
    out_other = flip(out_oth, "row")
    layer_out = jnp.concatenate(
        [jnp.where(row == 0, out_own, out_other), jnp.where(row == 0, out_other, out_own)], 0
    )

    def over_row(keep, send):
        return added(keep, flip(send, "row"))

    ffout_far = over_row(*outer_tall(hidden, 3, 3, 512, two_own, two_oth))
    ffout_far = flip(ffout_far, "col")
    ffout_near = over_row(*outer_tall(hidden, 0, 3, 512, two_own, two_oth))

    grad_pre, grad_one, one_own, one_oth, mixed_own, mixed_oth, sums_one, sums_inter = (
        chain_backward(vectors, grad_two, slope, normal_one, scale_one, weights)
    )
    inter_far = over_row(*outer_wide(normed, grad_pre, 3, 3, 512))
    attn_far = over_row(*outer_tall(parts[1][4], 0, 1, WIDE, one_own, one_oth))
    wide_far = flip(jnp.concatenate([inter_far, attn_far], 1), "col")
    inter_near = over_row(*outer_wide(normed, grad_pre, 0, 3, 512))
    attn_near = over_row(*outer_tall(parts[0][4], 0, 1, WIDE, one_own, one_oth))

    grad_ffout = sum_over_dp(added(ffout_near, ffout_far))
    grad_wide = sum_over_dp(added(jnp.concatenate([inter_near, attn_near], 1), wide_far))

    grads = [None, None]
    outer = [None, None]
    for side, grad_mixed in ((1, mixed_oth), (0, mixed_own)):
        pick, query, key, value, mixed, logsum = parts[side]
        grads[side] = attend_backward(pick, live, query, key, value, mixed, grad_mixed, logsum)
        keep, send, sums = outer_qkv(spot, both, *grads[side])
        outer[side] = (over_row(keep, send), sums)
    qkv_far = flip(outer[1][0], "col")
    grad_qkv = sum_over_dp(added(outer[0][0], qkv_far))

    near, away = unproject(
        spot,
        (grads[0][0], grads[1][0]),
        (grads[0][1], grads[1][1]),
        (grads[0][2], grads[1][2]),
        grad_one,
        (qkv_0, qkv_1, qkv_2, qkv_3),
    )
    grad_tokens = near + flip(away, "row").astype(F32)

    sums_qv = jnp.concatenate([outer[0][1], outer[1][1]], 1)
    summed = jnp.concatenate(
        [
            in_order(sums_qv[0], col),
            in_order(sums_qv[1], col),
            in_order(sums_one[2], row),
            in_order(sums_inter[0], col),
            in_order(sums_two[2], row),
            in_order(sums_one[0], row),
            in_order(sums_one[1], row),
            in_order(sums_two[0], row),
            in_order(sums_two[1], row),
        ]
    )
    summed = sum_everywhere(summed.reshape(-1, 128)).reshape(-1)
    vector_grads = []
    at = 0
    for width in (D, D, D, FF, D, D, D, D, D):
        vector_grads.append(summed[at : at + width])
        at += width
    grad_qkv = grad_qkv.astype(F32)
    return (
        layer_out,
        grad_tokens,
        grad_qkv[:, :WIDE],
        grad_qkv[:, WIDE : 2 * WIDE],
        grad_qkv[:, 2 * WIDE :],
        grad_wide[:, FH:].astype(F32),
        grad_wide[:, :FH].astype(F32),
        grad_ffout.astype(F32),
        *vector_grads,
    )


def solution(mesh):
    tokens = P(("dp", "col"), "row")
    down = P("row", "col")
    across = P("col", "row")
    return jax.shard_map(
        per_device,
        mesh=mesh,
        in_specs=(tokens, down, down, down, across, down, across) + (P(),) * 11 + (tokens,),
        out_specs=(tokens, tokens, down, down, down, across, down, across) + (P(),) * 9,
        check_vma=False,
    )
```
